32 devices in a mesh: shot: 4 (over y, core), recv: 8 (over z, x).
Axes of the slice: x: 2, y: 2, z: 4, core: 2. Of those that a mesh axis runs over, the one named last changes fastest.
Arguments:
- wavefield: bfloat16 [2, 8, 1, 1024, 4096], P(None, 'recv', None, None, 'shot'), may hold values from -1 to 1
- live: int32 [4096], replicated, may hold values 0 or 1
- block_order: int32 [32], replicated, may hold values from 0 to 31, each once
- wavelet: float32 [2, 2], replicated, may hold values from 0.5 to 1.5
Outputs:
- multiples: bfloat16 [2, 8, 1, 1024, 4096], P(None, 'recv', None, None, 'shot')
The draws below stay inside these ranges and needn't reach their ends.
Inputs may be any that keep to these rules, and one draw needn't show every extreme that they name: `block_order`: each block number appears once.
All inputs are finite; a program needn't handle non-finite values.
Results may differ from the reference program's by a relative error of at most 0.001.
Values may be sent and summed in bfloat16 or wider, within the bound.
No kernel may reach another device: no remote copies, remote signals or barrier semaphores. Data moves between devices by JAX's collectives and lax.ppermute only.
A program may use at most 64 MiB of HBM per device.

```python
import jax
import jax.numpy as jnp
from jax import lax

POINTS = 4096
BLOCK = 128
RGROUPS = 4
FREQ_DEV = 1
ROUNDS = 2
BPR = 2
NB = 32
FGROUPS = 2
FREQ = 2


def place_ends(values, key, least, top_value):
    dims = values.shape
    spot = [jax.random.randint(jax.random.fold_in(key, axis), (), 0, dims[axis]) for axis in range(len(dims))]
    values = values.at[tuple(spot)].set(least)
    longest = dims.index(max(dims))
    spot[longest] = (spot[longest] + 1) % dims[longest]
    return values.at[tuple(spot)].set(top_value)


def steps_of(rng, dims, split, smallest, largest):
    level, own = 1.0, jax.random.fold_in(rng, 6)
    for dim, blocks in split:
        steps = jnp.exp(jax.random.uniform(jax.random.fold_in(own, dim), (blocks,), jnp.float32, smallest / len(split), largest / len(split)))
        level = level * jnp.repeat(steps, dims[dim] // blocks).reshape([-1 if axis == dim else 1 for axis in range(len(dims))])
    return level


def centred(rng, shape, width, limit, cuts=(), kind=jnp.bfloat16):
    gain = steps_of(rng, shape, cuts, -0.22, 0.18) if cuts else 1.0
    array = jax.random.normal(rng, shape, jnp.float32) * width * gain
    return jnp.minimum(jnp.maximum(array, -limit), limit).astype(kind)


def setup_inputs(seed: int = 0) -> dict:
    arg_keys = jax.random.split(jax.random.key(seed), 5)
    return {
        "wavefield": centred(arg_keys[0], (2, FGROUPS * RGROUPS, FREQ_DEV, POINTS // RGROUPS, POINTS), 0.16, 1.0, ((1, 8), (4, 4))),
        "live": place_ends((jax.random.randint(arg_keys[1], (POINTS,), 0, 4) < 3).astype(jnp.int32), jax.random.fold_in(arg_keys[1], 1), 0, 1),
        "block_order": jax.random.permutation(arg_keys[2], NB).astype(jnp.int32),
        "wavelet": jnp.clip(jax.random.uniform(arg_keys[3], (2, FREQ), jnp.float32, 0.5, 1.5), 0.5, 1.5),
    }


def reference(wavefield, live, block_order, wavelet):
    groups = wavefield.shape[1] // RGROUPS
    rows = POINTS // RGROUPS
    chosen = block_order[:ROUNDS * BPR].astype(jnp.int32)
    index = (chosen[:, None] * BLOCK + jnp.arange(BLOCK, dtype=jnp.int32)[None, :]).reshape(-1).astype(jnp.int32)
    weight = jnp.take(live, index, axis=0).astype(wavefield.dtype)
    whole = wavefield.reshape(2, groups, RGROUPS, FREQ_DEV, rows, POINTS)
    whole = jnp.transpose(whole, (1, 3, 0, 2, 4, 5)).reshape(groups * FREQ_DEV, 2, POINTS, POINTS)

    def one_slice(args):
        slab, scale = args
        left = jnp.take(slab, index, axis=2)
        right = jnp.take(slab, index, axis=1) * weight[None, :, None]
        real = jnp.dot(left[0], right[0], preferred_element_type=jnp.float32) - jnp.dot(left[1], right[1], preferred_element_type=jnp.float32)
        imag = jnp.dot(left[0], right[1], preferred_element_type=jnp.float32) + jnp.dot(left[1], right[0], preferred_element_type=jnp.float32)
        out_re = -(scale[0] * real - scale[1] * imag)
        out_im = -(scale[0] * imag + scale[1] * real)
        return jnp.stack([out_re, out_im]).astype(jnp.bfloat16)

    result = lax.map(one_slice, (whole, jnp.transpose(wavelet)))
    result = result.reshape(groups, FREQ_DEV, 2, RGROUPS, rows, POINTS)
    result = jnp.transpose(result, (2, 0, 3, 1, 4, 5)).reshape(2, groups * RGROUPS, FREQ_DEV, rows, POINTS)
    return result
```

```python
import functools
import itertools

import jax
import jax.numpy as jnp
import numpy as np
from jax import lax
from jax.experimental import pallas as pl
from jax.experimental.pallas import tpu as pltpu
from jax.sharding import PartitionSpec as P

BLOCK = 128
RGROUPS = 4
ROUNDS = 2
BPR = 2
COUNT = ROUNDS * BPR


OWN, X1, Z1, X2, Z2, X3, Z3 = range(7)
PARTNER, Y1, E1, Y2, E2, Y3, E3 = range(1, 8)


def matched(missing, first, second):
    missing = sorted(missing)
    if len(missing) > 2:
        return None
    if not missing:
        return (None, None)
    if len(missing) == 1:
        b = missing[0]
        return (b, None) if b in first else (None, b) if b in second else None
    a, b = missing
    if a in first and b in second:
        return (a, b)
    if b in first and a in second:
        return (b, a)
    return None


def picks(missing, first, second):
    return [
        (a, b)
        for a in sorted(missing & first) or [None]
        for b in sorted(missing & second) or [None]
        if a != b or a is None
    ]


def row_schedule(owners):
    every = set(range(COUNT))
    own = [{b for b in every if owners[b] == d} for d in range(4)]
    firsts = [list(itertools.product(sorted(o) or [None], repeat=2)) for o in own]

    def gained(held, sent):
        return [held[d] | {sent[d ^ 1][0], sent[d ^ 2][1]} - {None} for d in range(4)]

    def turned(got):
        return [(got[d ^ 1][0], got[d ^ 2][1]) for d in range(4)]

    starts = [(sent, gained(own, sent)) for sent in itertools.product(*firsts)]
    for sent, held in starts:
        got = [matched(every - held[d], held[d ^ 1], held[d ^ 2]) for d in range(4)]
        if all(g is not None for g in got):
            return [sent, turned(got)]
    for sent, held in starts:
        options = [picks(every - held[d], held[d ^ 1], held[d ^ 2]) or [(None, None)] for d in range(4)]
        for got in itertools.product(*options):
            second = turned(got)
            after = gained(held, second)
            last = [matched(every - after[d], after[d ^ 1], after[d ^ 2]) for d in range(4)]
            if all(g is not None for g in last):
                return [sent, second, turned(last)]
    raise ValueError(owners)


@functools.cache
def row_table():
    table = np.zeros((RGROUPS**COUNT, RGROUPS, 3), np.int64)
    known = {}
    for owners in itertools.product(range(RGROUPS), repeat=COUNT):
        order = sorted(range(COUNT), key=lambda b: owners[b])
        key = tuple(owners[b] for b in order)
        if key not in known:
            known[key] = row_schedule(key)
        phases = [[tuple(None if b is None else order[b] for b in pair) for pair in sent] for sent in known[key]]
        where = [{b: OWN for b in range(COUNT) if owners[b] == d} for d in range(4)]
        sends = [[], [], [], []]
        for phase in range(3):
            sent = phases[phase] if phase < len(phases) else [(None, None)] * 4
            found = [dict(w) for w in where]
            for d in range(4):
                for axis in range(2):
                    b = sent[d][axis]
                    sends[d] += [0, 0] if b is None else [where[d][b], b]
                    if b is not None:
                        found[d ^ (1 << axis)].setdefault(b, (X1, X2, X3)[phase] + axis)
            where = found
        index = sum(o * RGROUPS**b for b, o in enumerate(owners))
        for d in range(4):
            for i, value in enumerate(sends[d][:8]):
                table[index, d, 0] |= value << 3 * i
            for i, value in enumerate(sends[d][8:] + [int(len(phases) > 2)]):
                table[index, d, 1] |= value << 3 * i
            for b in range(COUNT):
                table[index, d, 2] |= where[d][b] << 3 * b
    return table.astype(np.int32).reshape(-1)


@functools.cache
def column_table():
    table = np.zeros((4**COUNT, 4, 3), np.int64)
    for owners in itertools.product(range(4), repeat=COUNT):
        index = sum(o * 4**b for b, o in enumerate(owners))
        own = [[b for b in range(COUNT) if owners[b] == d] for d in range(4)]
        sent = [[None] * 3 for _ in range(4)]
        for chip in range(2):
            left = []
            for core in range(2):
                d = chip * 2 + core
                if own[d]:
                    sent[d][0] = own[d][0]
                left += own[d][1:]
            phase = 1
            while left:
                for core in range(2):
                    mine = [b for b in left if owners[b] == chip * 2 + core] or left
                    other = [b for b in left if owners[b] != chip * 2 + core]
                    b = mine[0] if mine and (owners[mine[0]] == chip * 2 + core or len(left) > 1 or core) else None
                    if core == 0 and b is not None and owners[b] != chip * 2 and not other:
                        b = None
                    if b is not None and left:
                        sent[chip * 2 + core][phase] = b
                        left.remove(b)
                    if not left:
                        break
                phase += 1
        for d in range(4):
            value = 0
            for phase in range(3):
                b = sent[d][phase]
                value |= (0 if b is None else b | int(owners[b] != d) << 2) << 3 * phase
            table[index, d, 0] = value
            table[index, d, 1] = int(any(s[2] is not None for s in sent))
            where = {}
            for b in range(COUNT):
                if owners[b] == d:
                    where[b] = OWN
                elif owners[b] == d ^ 1:
                    where[b] = PARTNER
                else:
                    for phase in range(3):
                        if sent[d ^ 2][phase] == b:
                            where[b] = (Y1, Y2, Y3)[phase]
                        elif sent[d ^ 3][phase] == b:
                            where[b] = (E1, E2, E3)[phase]
                table[index, d, 2] |= where[b] << 3 * b
    return table.astype(np.int32).reshape(-1)


def exchange(value, axis, bit):
    count = lax.axis_size(axis)
    return lax.ppermute(value, axis, [(low, low ^ bit) for low in range(count) if low ^ bit < count])


def field(word, i):
    return lax.bitwise_and(lax.shift_right_logical(word, 3 * i), 7)


def any_spec():
    return pl.BlockSpec(memory_space=pl.ANY)


def smem_spec():
    return pl.BlockSpec(memory_space=pltpu.SMEM)


def vmem_spec():
    return pl.BlockSpec(memory_space=pltpu.VMEM)


def choose(jobs):
    for cases, target, sem in jobs:
        for condition, source in cases:

            @pl.when(condition)
            def _(source=source, target=target, sem=sem):
                pltpu.make_async_copy(source, target, sem).start()

    for cases, target, sem in jobs:
        pltpu.make_async_copy(cases[0][1], target, sem).wait()


def rows_at(tile, order, b):
    start = lax.rem(order[b] * BLOCK, tile.shape[2])
    return tile.at[:, :, pl.ds(pl.multiple_of(start, BLOCK), BLOCK), :]


def columns_at(tile, order, b):
    start = lax.rem(order[b] * BLOCK, tile.shape[3])
    return tile.at[:, :, :, pl.ds(pl.multiple_of(start, BLOCK), BLOCK)]


def first_kernel(shot_plan, order, row_tab, col_tab, tile, x1, z1, y1, plan, sem):
    rows, cols = tile.shape[2], tile.shape[3]
    group = lax.rem(lax.axis_index("recv"), RGROUPS)
    pattern = 0
    for b in range(COUNT):
        pattern += lax.div(order[b] * BLOCK, rows) * RGROUPS**b
    base = (pattern * RGROUPS + group) * 3
    for w in range(3):
        plan[w] = row_tab[base + w]
    words = [row_tab[base + w] for w in range(3)]
    jobs = [
        ([(True, rows_at(tile, order, field(words[0], 1)))], x1, sem.at[0]),
        ([(True, rows_at(tile, order, field(words[0], 3)))], z1, sem.at[1]),
    ]
    if shot_plan:
        pattern = 0
        for b in range(COUNT):
            pattern += lax.div(order[b] * BLOCK, cols) * 4**b
        base = (pattern * 4 + lax.axis_index("shot")) * 3
        for w in range(3):
            plan[3 + w] = col_tab[base + w]
        jobs.append(([(True, columns_at(tile, order, field(col_tab[base], 0)))], y1, sem.at[2]))
    else:
        plan[3] = 0
        plan[4] = 0
        plan[5] = sum(PARTNER << 3 * b for b in range(COUNT))
    choose_plain(jobs)


def choose_plain(jobs):
    for cases, target, sem in jobs:
        pltpu.make_async_copy(cases[0][1], target, sem).start()
    for cases, target, sem in jobs:
        pltpu.make_async_copy(cases[0][1], target, sem).wait()


def own_kernel(order, tile, out, sem):
    jobs = [([(True, columns_at(tile, order, b))], out.at[b], sem.at[b]) for b in range(COUNT)]
    choose_plain(jobs)


def column_kernel(phase, order, plan, tile, partner, out, sem):
    code = field(plan[3], phase)
    b = lax.bitwise_and(code, 3)
    choose([([(code < 4, columns_at(tile, order, b)), (code >= 4, partner.at[b])], out, sem.at[0])])


def row_kernel(phase, order, plan, tile, *refs):
    slots, (x, z, sem) = refs[:-3], refs[-3:]
    jobs = []
    for axis, out in enumerate((x, z)):
        word, at = (plan[0], 4 + 2 * axis) if phase == 1 else (plan[1], 2 * axis)
        slot, b = field(word, at), field(word, at + 1)
        cases = [(slot == OWN, rows_at(tile, order, b))]
        cases += [(slot == 1 + i, ref) for i, ref in enumerate(slots)]
        jobs.append((cases, out, sem.at[axis]))
    choose(jobs)


def product_kernel(n_rows, n_cols, order, plan, scales, mask, tile, *refs):
    row_slots, partner, col_slots = refs[:n_rows], refs[n_rows], refs[n_rows + 1 : n_rows + 1 + n_cols]
    out, left, right, sem = refs[n_rows + 1 + n_cols :]
    freqs = tile.shape[1]
    step = pl.program_id(0)
    tn = out.shape[-1]

    @pl.when(step == 0)
    def _():
        jobs = []
        for b in range(COUNT):
            slot = field(plan[2], b)
            cases = [(slot == OWN, rows_at(tile, order, b))]
            cases += [(slot == 1 + i, ref) for i, ref in enumerate(row_slots)]
            jobs.append((cases, right.at[b], sem.at[b]))
            slot = field(plan[5], b)
            cases = [(slot == OWN, columns_at(tile, order, b)), (slot == PARTNER, partner.at[b])]
            cases += [(slot == 2 + i, ref) for i, ref in enumerate(col_slots)]
            jobs.append((cases, left.at[b], sem.at[COUNT + b]))
        choose(jobs)

    at = pl.ds(pl.multiple_of(step * tn, tn), tn)
    for f in range(freqs):
        lhs = jnp.concatenate([left[b, part, f] for b in range(COUNT) for part in range(2)], axis=1)
        res, ims = [], []
        for b in range(COUNT):
            live = jnp.concatenate([mask[b]] * (tn // BLOCK), axis=1)
            re = right[b, 0, f, :, at] * live
            im = right[b, 1, f, :, at] * live
            res += [re, -im]
            ims += [im, re]
        real = jnp.dot(lhs, jnp.concatenate(res, axis=0), preferred_element_type=jnp.float32)
        imag = jnp.dot(lhs, jnp.concatenate(ims, axis=0), preferred_element_type=jnp.float32)
        s_re, s_im = scales[0, f], scales[1, f]
        out[0, f] = (-(s_re * real - s_im * imag)).astype(out.dtype)
        out[1, f] = (-(s_re * imag + s_im * real)).astype(out.dtype)


def shards(wavefield, live, block_order, wavelet):
    tile = wavefield[:, 0]
    _, freqs, rows, cols = tile.shape
    kind = tile.dtype
    order = block_order[:COUNT]
    freq_group = lax.axis_index("recv") // RGROUPS
    scales = lax.dynamic_slice_in_dim(wavelet, freq_group * freqs, freqs, 1)
    shot_plan = lax.axis_size("shot") == 4
    row_block = jax.ShapeDtypeStruct((2, freqs, BLOCK, cols), kind)
    col_block = jax.ShapeDtypeStruct((2, freqs, rows, BLOCK), kind)
    col_blocks = jax.ShapeDtypeStruct((COUNT, 2, freqs, rows, BLOCK), kind)

    def call(kernel, n_smem, outs, n_sem, *args):
        return pl.pallas_call(
            kernel,
            out_shape=outs,
            in_specs=[smem_spec()] * n_smem + [any_spec()] * (len(args) - n_smem),
            out_specs=jax.tree.map(lambda o: smem_spec() if o.dtype == jnp.int32 else vmem_spec(), outs),
            scratch_shapes=[pltpu.SemaphoreType.DMA((n_sem,))],
        )(*args)

    x1, z1, y1, plan = call(
        functools.partial(first_kernel, shot_plan),
        3,
        (row_block, row_block, col_block, jax.ShapeDtypeStruct((8,), jnp.int32)),
        3,
        order,
        jnp.asarray(row_table()),
        jnp.asarray(column_table()),
        tile,
    )
    x1 = exchange(x1, "recv", 1)
    z1 = exchange(z1, "recv", 2)
    mine = call(own_kernel, 1, col_blocks, COUNT, order, tile)
    if shot_plan:
        y1 = exchange(y1, "shot", 2)
        partner = exchange(mine, "shot", 1)
        y2 = call(functools.partial(column_kernel, 1), 2, col_block, 1, order, plan, tile, partner)
        y2 = exchange(y2, "shot", 2)
        e1 = exchange(y1, "shot", 1)
        e2 = exchange(y2, "shot", 1)
        col_slots = (y1, e1, y2, e2)
    else:
        holder = order * BLOCK // cols
        mine = jnp.where((holder == lax.axis_index("shot"))[:, None, None, None, None], mine, jnp.zeros_like(mine))
        partner = lax.psum(mine, "shot")
        col_slots = ()
    x2, z2 = call(functools.partial(row_kernel, 1), 2, (row_block, row_block), 2, order, plan, tile, x1, z1)
    x2 = exchange(x2, "recv", 1)
    z2 = exchange(z2, "recv", 2)
    row_slots = (x1, z1, x2, z2)

    weight = jnp.take(live.reshape(-1, BLOCK), order, axis=0).astype(kind)
    mask = jnp.broadcast_to(weight[:, :, None], (COUNT, BLOCK, BLOCK))

    def product(row_slots, col_slots):
        tn = min(cols, 256)
        return pl.pallas_call(
            functools.partial(product_kernel, len(row_slots), len(col_slots)),
            grid=(cols // tn,),
            out_shape=jax.ShapeDtypeStruct(tile.shape, kind),
            in_specs=[smem_spec()] * 3
            + [vmem_spec()]
            + [any_spec()] * (2 + len(row_slots) + len(col_slots)),
            out_specs=pl.BlockSpec((2, freqs, rows, tn), lambda n: (0, 0, 0, n)),
            scratch_shapes=[
                pltpu.VMEM(col_blocks.shape, kind),
                pltpu.VMEM((COUNT, *row_block.shape), kind),
                pltpu.SemaphoreType.DMA((2 * COUNT,)),
            ],
        )(order, plan, scales, mask, tile, *row_slots, partner, *col_slots)

    def longer(row_slots, col_slots):
        x3, z3 = call(functools.partial(row_kernel, 2), 2, (row_block, row_block), 2, order, plan, tile, *row_slots)
        x3 = exchange(x3, "recv", 1)
        z3 = exchange(z3, "recv", 2)
        if col_slots:
            y3 = call(functools.partial(column_kernel, 2), 2, col_block, 1, order, plan, tile, partner)
            y3 = exchange(y3, "shot", 2)
            e3 = exchange(y3, "shot", 1)
            col_slots = (*col_slots, y3, e3)
        return product((*row_slots, x3, z3), col_slots)

    again = (field(plan[1], 4) + plan[4]) > 0
    result = lax.cond(again, longer, product, row_slots, col_slots)
    return result[:, None]


def solution(mesh):
    placed = (P(None, "recv", None, None, "shot"), P(), P(), P())
    return jax.shard_map(
        shards,
        mesh=mesh,
        in_specs=placed,
        out_specs=P(None, "recv", None, None, "shot"),
        check_vma=False,
    )
```

```python
import functools
import itertools

import jax
import jax.numpy as jnp
import numpy as np
from jax import lax
from jax.experimental import pallas as pl
from jax.experimental.pallas import tpu as pltpu
from jax.sharding import PartitionSpec as P

BLOCK = 128
RGROUPS = 4
ROUNDS = 2
BPR = 2
COUNT = ROUNDS * BPR


OWN, X1, Z1, X2, Z2, HALVES3 = range(6)
X3, Z3 = 5, 6
PARTNER, Y1, E1, HALVESY2, HALVESY3, Y3, E3 = range(1, 8)


def matched(missing, first, second):
    missing = sorted(missing)
    for a in [None, *missing]:
        for b in [None, *missing]:
            if set(missing) <= {a, b} and (a is None or a in first) and (b is None or b in second):
                return (a, b)
    return None


def turned(got):
    return [(got[d ^ 1][0], got[d ^ 2][1]) for d in range(4)]


def row_schedule(owners):
    every = set(range(COUNT))
    own = [[b for b in range(COUNT) if owners[b] == d] for d in range(4)]
    first = [(o[0], o[min(1, len(o) - 1)]) if o else (None, None) for o in own]

    def gained(held, sent):
        return [held[d] | ({sent[d ^ 1][0], sent[d ^ 2][1]} - {None}) for d in range(4)]

    none = [(None, None)] * 4
    held = gained([set(o) for o in own], first)
    got = [matched(every - held[d], held[d ^ 1], held[d ^ 2]) for d in range(4)]
    if all(g is not None for g in got):
        return first, turned(got), none, none, 0
    options = [
        list(itertools.product(*([*sorted((every - held[d]) & held[d ^ n]), None] for n in (1, 2)))) for d in range(4)
    ]
    best = None
    for got in itertools.product(*options):
        second = turned(got)
        after = gained(held, second)
        missing = [every - after[d] for d in range(4)]
        last = [matched(missing[d], after[d ^ 1], after[d ^ 2]) for d in range(4)]
        if any(g is None for g in last):
            continue
        if all(len(m) <= 1 and m <= after[d ^ 1] and m <= after[d ^ 2] for d, m in enumerate(missing)):
            halves = [(*m, *m) if m else (None, None) for m in missing]
            return first, second, turned(halves), turned(last), 1
        best = best or (first, second, none, turned(last), 2)
    return best


@functools.cache
def row_table():
    table = np.zeros((RGROUPS**COUNT, RGROUPS, 4), np.int64)
    for owners in itertools.product(range(RGROUPS), repeat=COUNT):
        first, second, halves, whole, kind = row_schedule(owners)
        index = sum(o * RGROUPS**b for b, o in enumerate(owners))
        where = [{b: OWN for b in range(COUNT) if owners[b] == d} for d in range(4)]

        def move(where, sent, codes):
            found = [dict(w) for w in where]
            sends = [[] for _ in range(4)]
            for d in range(4):
                for axis, b in enumerate(sent[d]):
                    sends[d] += [0, 0] if b is None else [where[d][b], b]
                    if b is not None:
                        found[d ^ (1 << axis)].setdefault(b, codes[axis])
            return found, sends

        where, _ = move(where, first, (X1, Z1))
        where, sends = move(where, second, (X2, Z2))
        where1, sends1 = move(where, halves, (HALVES3, HALVES3))
        where2, sends2 = move(where, whole, (X3, Z3))
        for d in range(4):
            words = (
                sends[d] + sends1[d],
                [*sends2[d], kind],
                [where1[d].get(b, OWN) for b in range(COUNT)],
                [where2[d][b] for b in range(COUNT)],
            )
            for w, values in enumerate(words):
                table[index, d, w] = sum(value << 3 * i for i, value in enumerate(values))
    return table.astype(np.int32).reshape(-1)


@functools.cache
def column_table():
    table = np.zeros((4**COUNT, 4, 4), np.int64)
    for owners in itertools.product(range(4), repeat=COUNT):
        index = sum(o * 4**b for b, o in enumerate(owners))
        own = [[b for b in range(COUNT) if owners[b] == d] for d in range(4)]
        left = [own[2 * chip][1:] + own[2 * chip + 1][1:] for chip in range(2)]
        kind = max(0, max(len(rest) for rest in left) - 1)
        for d in range(4):
            rest = left[d // 2]
            sends = [rest[0] if rest else None, rest[1] if len(rest) > 1 else None, None]
            sends[2] = (rest[1:] + [None, None])[d % 2]
            words = [sum(0 if b is None else (b | (owners[b] != d) << 2) << 3 * i for i, b in enumerate(sends)), kind, 0, 0]
            rest = left[1 - d // 2]
            for b in range(COUNT):
                if owners[b] == d:
                    codes = (OWN, OWN)
                elif owners[b] == d ^ 1:
                    codes = (PARTNER, PARTNER)
                elif b not in rest:
                    codes = (Y1, Y1) if owners[b] == d ^ 2 else (E1, E1)
                elif b == rest[0]:
                    codes = (HALVESY2, HALVESY2)
                else:
                    codes = (HALVESY3, Y3 if rest.index(b) - 1 == d % 2 else E3)
                words[2] |= codes[0] << 3 * b
                words[3] |= codes[1] << 3 * b
            table[index, d] = words
    return table.astype(np.int32).reshape(-1)


ANY = pl.BlockSpec(memory_space=pl.ANY)
HBM = pl.BlockSpec(memory_space=pltpu.HBM)
VMEM = pl.BlockSpec(memory_space=pltpu.VMEM)
SMEM = pl.BlockSpec(memory_space=pltpu.SMEM)


def exchange(value, axis, bit):
    count = lax.axis_size(axis)
    return lax.ppermute(value, axis, [(low, low ^ bit) for low in range(count) if low ^ bit < count])


def field(word, i):
    return lax.bitwise_and(lax.shift_right_logical(word, 3 * i), 7)


def offset(block, size):
    return pl.multiple_of(lax.rem(block * BLOCK, size), BLOCK)


def copy_all(copies):
    for copy in copies:
        copy.start()
    for copy in copies:
        copy.wait()


def first_two(order, size, me):
    first, second, found = order[0], order[0], 0
    for b in range(COUNT):
        mine = lax.div(order[b] * BLOCK, size) == me
        first = jnp.where(mine & (found == 0), order[b], first)
        second = jnp.where(mine & (found < 2), order[b], second)
        found = found + mine.astype(jnp.int32)
    return first, second


def first_kernel(order, tile, x1a, z1a, x1b, z1b, *rest):
    sem = rest[-1]
    rows, cols = tile.shape[2], tile.shape[3]
    near = x1a.shape[-1]
    group = lax.rem(lax.axis_index("recv"), RGROUPS)
    copies = []
    for block, left, right in zip(first_two(order, rows, group), (x1a, z1a), (x1b, z1b), strict=True):
        span = pl.ds(offset(block, rows), BLOCK)
        copies.append((tile.at[:, :, span, :near], left))
        copies.append((tile.at[:, :, span, near:], right))
    if len(rest) > 1:
        block, _ = first_two(order, cols, lax.axis_index("shot"))
        copies.append((tile.at[:, :, :, pl.ds(offset(block, cols), BLOCK)], rest[0]))
    copy_all([pltpu.make_async_copy(src, dst, sem.at[i]) for i, (src, dst) in enumerate(copies)])


def own_kernel(shot_plan, order, row_tab, col_tab, tile, sent, own_cols, own_rows, plan, kind, sem):
    rows, cols = tile.shape[2], tile.shape[3]
    copies = []
    for b in range(COUNT):
        copies.append((tile.at[:, :, :, pl.ds(offset(order[b], cols), BLOCK)], own_cols.at[b]))
        copies.append((tile.at[:, :, pl.ds(offset(order[b], rows), BLOCK), :], own_rows.at[b]))
    copies = [pltpu.make_async_copy(src, dst, sem.at[i]) for i, (src, dst) in enumerate(copies)]
    for copy in copies:
        copy.start()
    pattern = sum(lax.div(order[b] * BLOCK, rows) * RGROUPS**b for b in range(COUNT))
    base = (pattern * RGROUPS + lax.rem(lax.axis_index("recv"), RGROUPS)) * 4
    for w in range(4):
        plan[w] = row_tab[base + w]
    most = field(row_tab[base + 1], 4)
    if shot_plan:
        pattern = sum(lax.div(order[b] * BLOCK, cols) * 4**b for b in range(COUNT))
        base = (pattern * 4 + lax.axis_index("shot")) * 4
        for w in range(4):
            plan[4 + w] = col_tab[base + w]
        most = jnp.maximum(most, col_tab[base + 1])
    else:
        for w, value in enumerate((0, 0, PARTNER, PARTNER)):
            plan[4 + w] = value * sum(1 << 3 * b for b in range(COUNT))
    kind[0] = most
    for copy in copies:
        copy.wait()


class Rows:
    def __init__(self, own, x1, z1, x2=None, z2=None, third=()):
        self.own = own
        self.pieces = {}
        for code, parts in ((X1, x1), (Z1, z1), (X2, x2), (Z2, z2), *third):
            if parts is not None:
                self.pieces[code] = parts

    def pick(self, code, b, low, high, put):
        @pl.when(code == OWN)
        def _():
            put(low, high, lambda p, f: self.own[b, p, f, :, low:high])

        for at, parts in self.pieces.items():

            @pl.when(code == at)
            def _(parts=parts):
                for start, stop, ref in parts:
                    lo, hi = max(low, start), min(high, stop)
                    if lo < hi:
                        put(lo, hi, lambda p, f: ref[p, f, :, lo - start : hi - start])


def send_rows(rows, plan, word, at, spans, outs):
    for axis, (out, (low, high)) in enumerate(zip(outs, spans, strict=True)):
        code, b = field(plan[word], at + 2 * axis), field(plan[word], at + 2 * axis + 1)

        def put(lo, hi, load):
            for p in range(out.shape[0]):
                for f in range(out.shape[1]):
                    out[p, f, :, lo - low : hi - low] = load(p, f)

        rows.pick(code, b, low, high, put)


def second_kernel(low, high, plan, own, x1, z1, x2, z2):
    rows = Rows(own, [(low, high, x1)], [(low, high, z1)])
    send_rows(rows, plan, 0, 0, [(low, high)] * 2, (x2, z2))


def third_kernel(halves, near, plan, own, *refs):
    parts, outs = refs[:8], refs[8:]
    cols = own.shape[-1]
    rows = Rows(own, *([(0, near, a), (near, cols, b)] for a, b in zip(parts[::2], parts[1::2], strict=True)))
    if halves:
        send_rows(rows, plan, 0, 4, [(0, cols // 2), (cols // 2, cols)], outs)
    else:
        send_rows(rows, plan, 1, 0, [(0, cols)] * 2, outs)


def column_kernel(phase, plan, own, partner, out):
    code = field(plan[4], phase)
    b = lax.bitwise_and(code, 3)
    rows = out.shape[2]
    half = lax.rem(lax.axis_index("shot"), 2) if rows < own.shape[3] else 0
    span = pl.ds(pl.multiple_of(half * rows, rows), rows)
    for condition, ref in ((code < 4, own), (code >= 4, partner)):

        @pl.when(condition)
        def _(ref=ref):
            for p in range(out.shape[0]):
                for f in range(out.shape[1]):
                    out[p, f] = ref[b, p, f, span, :]


def fill_left(left, order, word, live, own, partner, slots):
    rows = left.shape[1]
    core = lax.rem(lax.axis_index("shot"), 2)
    for b in range(COUNT):
        code = field(word, b)
        weight = live[pl.ds(order[b], 1), :].astype(left.dtype)

        def put(load, span, b=b, weight=weight):
            for f in range(left.shape[0]):
                for p in range(2):
                    at = (2 * b + p) * BLOCK
                    left[f, span, at : at + BLOCK] = load(p, f) * weight

        @pl.when(code == OWN)
        def _():
            put(lambda p, f: own[b, p, f], slice(None))

        @pl.when(code == PARTNER)
        def _():
            put(lambda p, f: partner[b, p, f], slice(None))

        for at, refs in slots.items():

            @pl.when(code == at)
            def _(refs=refs):
                if isinstance(refs, tuple):
                    for half, ref in zip((core, 1 - core), refs, strict=True):
                        span = pl.ds(pl.multiple_of(half * (rows // 2), rows // 2), rows // 2)
                        put(lambda p, f: ref[p, f], span)
                else:
                    put(lambda p, f: refs[p, f], slice(None))


def fill_right(right, word, rows, low, high):
    width = high - low
    for b in range(COUNT):

        def put(lo, hi, load, b=b):
            top, bottom = slice(2 * b * BLOCK, (2 * b + 1) * BLOCK), slice((2 * b + 1) * BLOCK, (2 * b + 2) * BLOCK)
            here, there = slice(lo - low, hi - low), slice(width + lo - low, width + hi - low)
            for f in range(right.shape[0]):
                re, im = load(0, f), load(1, f)
                right[f, top, here] = re
                right[f, bottom, there] = re
                right[f, top, there] = im
                right[f, bottom, here] = -im

        rows.pick(field(word, b), b, low, high, put)


def multiply(wavelet, left, right, out):
    freqs, tn = out.shape[1], out.shape[-1]
    width = right.shape[-1] // 2
    at = pl.program_id(0) * tn
    group = lax.div(lax.axis_index("recv"), RGROUPS)
    for f in range(freqs):
        real, imag = (
            jnp.dot(
                left[f], right[f, :, pl.ds(pl.multiple_of(at + start, tn), tn)], preferred_element_type=jnp.float32
            )
            for start in (0, width)
        )
        s_re, s_im = wavelet[0, group * freqs + f], wavelet[1, group * freqs + f]
        out[0, f] = (-(s_re * real - s_im * imag)).astype(out.dtype)
        out[1, f] = (-(s_re * imag + s_im * real)).astype(out.dtype)


def near_kernel(order, plan, wavelet, live, own_rows, own_cols, partner, x1, z1, x2, z2, *refs):
    *slots, out, left, right = refs
    high = x1.shape[-1]

    @pl.when(pl.program_id(0) == 0)
    def _():
        codes = {}
        if slots:
            codes = {Y1: slots[0], E1: slots[1], HALVESY2: (slots[2], slots[3])}
        fill_left(left, order, plan[6], live, own_cols, partner, codes)
        rows = Rows(own_rows, *([(0, high, ref)] for ref in (x1, z1, x2, z2)))
        fill_right(right, plan[2], rows, 0, high)

    multiply(wavelet, left, right, out)


def far_kernel(plan, wavelet, own_rows, left, x1, z1, x2, z2, held, out, right):
    high = own_rows.shape[-1]
    low = high - x1.shape[-1]

    @pl.when(pl.program_id(0) == 0)
    def _():
        rows = Rows(own_rows, *([(low, high, ref)] for ref in (x1, z1, x2, z2)))
        fill_right(right, plan[2], rows, low, high)

    multiply(wavelet, left, right, out)


def late_kernel(halves, near, order, plan, wavelet, live, own_rows, own_cols, partner, *refs):
    parts, x3, z3, *slots, held, out, left, right = refs[:8], *refs[8:]
    cols = own_rows.shape[-1]

    @pl.when(pl.program_id(0) == 0)
    def _():
        codes = {}
        if slots:
            codes = {Y1: slots[0], E1: slots[1], HALVESY2: (slots[2], slots[3])}
            codes.update({HALVESY3: (slots[4], slots[5])} if halves else {Y3: slots[4], E3: slots[5]})
        fill_left(left, order, plan[6 if halves else 7], live, own_cols, partner, codes)
        if halves:
            third = [(HALVES3, [(0, cols // 2, x3), (cols // 2, cols, z3)])]
        else:
            third = [(X3, [(0, cols, x3)]), (Z3, [(0, cols, z3)])]
        pairs = zip(parts[::2], parts[1::2], strict=True)
        rows = Rows(own_rows, *([(0, near, a), (near, cols, b)] for a, b in pairs), third=third)
        fill_right(right, plan[2 if halves else 3], rows, 0, cols)

    multiply(wavelet, left, right, out)


def shards(wavefield, live, block_order, wavelet):
    tile = wavefield[:, 0]
    _, freqs, rows, cols = tile.shape
    kind = tile.dtype
    tn = min(cols // 2, 2 * BLOCK)
    near = max(tn, cols * 5 // 8 // tn * tn)
    shot_plan = lax.axis_size("shot") == 4
    live = live.reshape(-1, BLOCK)

    def array(*shape, dtype=kind):
        return jax.ShapeDtypeStruct(shape, dtype)

    def row_block(width):
        return array(2, freqs, BLOCK, width)

    def col_block(height):
        return array(2, freqs, height, BLOCK)

    def call(kernel, outs, ins, args, scratch=(), mib=8):
        return pl.pallas_call(
            kernel,
            out_shape=jax.tree.map(lambda o: o if o.dtype == jnp.int32 else pltpu.VMEM(o.shape, o.dtype), outs),
            in_specs=ins,
            out_specs=jax.tree.map(lambda o: SMEM if o.dtype == jnp.int32 else VMEM, outs),
            scratch_shapes=scratch,
            compiler_params=pltpu.CompilerParams(vmem_limit_bytes=mib << 20),
        )(*args)

    firsts = [row_block(near)] * 2 + [row_block(cols - near)] * 2 + [col_block(rows)] * shot_plan
    source = pltpu.with_memory_space_constraint(tile, pltpu.HBM)
    x1a, z1a, x1b, z1b, *y1 = call(
        first_kernel, firsts, [SMEM, HBM], (block_order, source), [pltpu.SemaphoreType.DMA((5,))]
    )
    sent = x1a
    x1a, z1a, x1b, z1b = exchange(x1a, "recv", 1), exchange(z1a, "recv", 2), exchange(x1b, "recv", 1), exchange(z1b, "recv", 2)
    own_cols, own_rows, plan, most = call(
        functools.partial(own_kernel, shot_plan),
        [array(COUNT, 2, freqs, rows, BLOCK), array(COUNT, 2, freqs, BLOCK, cols), array(8, dtype=jnp.int32), array(1, dtype=jnp.int32)],
        [SMEM] * 3 + [HBM, VMEM],
        (block_order, jnp.asarray(row_table()), jnp.asarray(column_table()), source, sent),
        [pltpu.SemaphoreType.DMA((2 * COUNT,))],
    )
    if shot_plan:
        y1 = exchange(y1[0], "shot", 2)
        partner = exchange(own_cols, "shot", 1)

        def send_columns(phase, height):
            y = call(functools.partial(column_kernel, phase), col_block(height), [SMEM, VMEM, VMEM], (plan, own_cols, partner))
            y = exchange(y, "shot", 2)
            return y, exchange(y, "shot", 1)

        col_slots = (y1, exchange(y1, "shot", 1), *send_columns(0, rows // 2))
    else:
        holder = block_order[:COUNT] * BLOCK // cols
        mine = (holder == lax.axis_index("shot"))[:, None, None, None, None]
        partner = lax.psum(jnp.where(mine, own_cols, jnp.zeros_like(own_cols)), "shot")
        col_slots = ()

    def send_rows_second(low, high, x1, z1):
        outs = [row_block(high - low)] * 2
        x2, z2 = call(functools.partial(second_kernel, low, high), outs, [SMEM] + [VMEM] * 3, (plan, own_rows, x1, z1))
        return exchange(x2, "recv", 1), exchange(z2, "recv", 2)

    x2a, z2a = send_rows_second(0, near, x1a, z1a)
    x2b, z2b = send_rows_second(near, cols, x1b, z1b)

    def product(kernel, low, high, smem, vmem, held=None, make_left=True):
        outs, out_specs = [pltpu.HBM(tile.shape, kind)], [pl.BlockSpec((2, freqs, rows, tn), lambda n: (0, 0, 0, n + low // tn))]
        left = array(freqs, rows, 2 * COUNT * BLOCK)
        keep = held is None
        scratch = [pltpu.VMEM((freqs, 2 * COUNT * BLOCK, 2 * (high - low)), kind)]
        if keep:
            outs.append(pltpu.VMEM(left.shape, kind))
            out_specs.append(VMEM)
        elif make_left:
            scratch.insert(0, pltpu.VMEM(left.shape, kind))
        args = (*smem, *vmem, *(() if keep else (held,)))
        return pl.pallas_call(
            kernel,
            grid=((high - low) // tn,),
            out_shape=outs,
            in_specs=[SMEM] * len(smem) + [VMEM] * len(vmem) + ([] if keep else [ANY]),
            out_specs=out_specs,
            scratch_shapes=scratch,
            input_output_aliases={} if keep else {len(args) - 1: 0},
            cost_estimate=pl.CostEstimate(
                flops=16 * freqs * rows * COUNT * BLOCK * (high - low) // 2,
                bytes_accessed=4 * freqs * rows * (high - low) * 2,
                transcendentals=0,
            ),
            compiler_params=pltpu.CompilerParams(vmem_limit_bytes=28 << 20),
        )(*args)

    ahead = (block_order, plan, wavelet)
    held, left = product(
        near_kernel, 0, near, ahead, (live, own_rows, own_cols, partner, x1a, z1a, x2a, z2a, *col_slots)
    )
    parts = (x1a, x1b, z1a, z1b, x2a, x2b, z2a, z2b)

    def done(held):
        return product(far_kernel, near, cols, (plan, wavelet), (own_rows, left, x1b, z1b, x2b, z2b), held, False)[0]

    def again(halves, held):
        width, height = (cols // 2, rows // 2) if halves else (cols, rows)
        kernel = functools.partial(third_kernel, halves, near)
        x3, z3 = call(kernel, [row_block(width)] * 2, [SMEM] + [VMEM] * 9, (plan, own_rows, *parts))
        x3, z3 = exchange(x3, "recv", 1), exchange(z3, "recv", 2)
        slots = (*col_slots, *send_columns(1 if halves else 2, height)) if shot_plan else ()
        kernel = functools.partial(late_kernel, halves, near)
        return product(kernel, 0, cols, ahead, (live, own_rows, own_cols, partner, *parts, x3, z3, *slots), held)[0]

    branches = (done, functools.partial(again, True), functools.partial(again, False))
    return lax.switch(most[0], branches, held)[:, None]


def solution(mesh):
    placed = (P(None, "recv", None, None, "shot"), P(), P(), P())
    return jax.shard_map(
        shards,
        mesh=mesh,
        in_specs=placed,
        out_specs=P(None, "recv", None, None, "shot"),
        check_vma=False,
    )
```
